256 devices in a mesh: gx: 64 (over z_lo, y, x), gz: 4 (over z_hi, core).
Axes of the slice: x: 4, y: 4, z: 8 (z_hi: 2, z_lo: 4; z = z_hi * 4 + z_lo), core: 2. Of those that a mesh axis runs over, the one named last changes fastest.
Arguments:
- tracer: float32 [2, 100, 16, 8192], P(None, 'gz', None, 'gx'), may hold values from -6 to 6
- east_flow: float32 [100, 16, 8192], P('gz', None, 'gx'), may hold values from -0.35 to 0.35
- north_flow: float32 [100, 16, 8192], P('gz', None, 'gx'), may hold values from -0.35 to 0.35
- vertical_flow: float32 [100, 16, 8192], P('gz', None, 'gx'), may hold values from -0.3 to 0.3
- mixing_lateral: float32 [100, 16, 8192], P('gz', None, 'gx'), may hold values from 0.02 to 0.12
- mixing_vertical: float32 [100, 16, 8192], P('gz', None, 'gx'), may hold values from 0.5 to 500
- sea_mask: int32 [100, 16, 8192], P('gz', None, 'gx'), may hold values 0 or 1
- bottom: int32 [16, 8192], P(None, 'gx'), may hold values from 25 to 100
Outputs:
- updated: float32 [2, 100, 16, 8192], P(None, 'gz', None, 'gx')
The draws below stay inside these ranges and needn't reach their ends.
All inputs are finite; a program needn't handle non-finite values. No bound on the sum of `sea_mask` on one device may be relied on, other than what follows from the above.
Results may differ from the reference program's by a relative error of at most 0.000032.
Values sent between devices are 32-bit elements; how exact they have to be, the bound alone decides.
A program may use at most 64 MiB of HBM per device.

```python
import math
import jax
import jax.numpy as jnp
from jax import lax

NTR = 2
LEV = 100
SUB = 3
NY = 16
NX = 8192


def place_ends(values, key, least, top_value):
    index_at = [jax.random.randint(jax.random.fold_in(key, axis), (), 0, length) for axis, length in enumerate(values.shape)]
    longest = values.shape.index(max(values.shape))
    neighbour = index_at[:longest] + [(index_at[longest] + 1) % values.shape[longest]] + index_at[longest + 1:]
    return values.at[tuple(index_at)].set(least).at[tuple(neighbour)].set(top_value)


def level_of(rng, shape, shards, low, top_value):
    def one(position, shards_of):
        steps = jax.random.uniform(jax.random.fold_in(jax.random.fold_in(rng, 6), position), (shards_of,), jnp.float32, low / len(shards), top_value / len(shards))
        return jnp.repeat(jnp.exp(steps), shape[position] // shards_of).reshape((-1,) + (1,) * (len(shape) - position - 1))

    level = one(*shards[0])
    for cut in shards[1:]:
        level = level * one(*cut)
    return level


def gaussian(own_key, dims, deviation, most, pieces=(), kind=jnp.bfloat16):
    drawn = jax.random.normal(own_key, dims, jnp.float32) * deviation
    if len(pieces) > 0:
        drawn = level_of(own_key, dims, pieces, -0.22, 0.18) * drawn
    return jnp.clip(drawn, min=-most, max=most).astype(kind)


def setup_inputs(seed: int = 0) -> dict:
    seeds = jax.random.split(jax.random.key(seed), 9)
    tracer = gaussian(seeds[0], (NTR, LEV, NY, NX), 1.0, 6.0, ((1, 4), (3, 64)), jnp.float32)
    east_flow = jnp.clip(jax.random.uniform(seeds[1], (LEV, NY, NX), jnp.float32, -0.35, 0.35) * level_of(seeds[1], (LEV, NY, NX), ((0, 4), (2, 64)), -0.4, 0.0), -0.35, 0.35)
    north_flow = jnp.clip(jax.random.uniform(seeds[2], (LEV, NY, NX), jnp.float32, -0.35, 0.35) * level_of(seeds[2], (LEV, NY, NX), ((0, 4), (2, 64)), -0.4, 0.0), -0.35, 0.35)
    vertical_flow = jnp.clip(jax.random.uniform(seeds[3], (LEV, NY, NX), jnp.float32, -0.3, 0.3) * level_of(seeds[3], (LEV, NY, NX), ((0, 4), (2, 64)), -0.4, 0.0), -0.3, 0.3)
    mixing_lateral = jnp.clip(jnp.exp(math.log(0.12) - 1.7917595 * jax.random.uniform(seeds[4], (LEV, NY, NX), jnp.float32) ** level_of(seeds[4], (LEV, NY, NX), ((0, 4), (2, 64)), -0.2, 0.2)), 0.02, 0.12)
    mixing_vertical = jnp.clip(jnp.exp(math.log(500.0) - 6.9077553 * jax.random.uniform(seeds[5], (LEV, NY, NX), jnp.float32) ** level_of(seeds[5], (LEV, NY, NX), ((0, 4), (2, 64)), -0.2, 0.2)), 0.5, 500.0)
    sea_mask = place_ends((jax.random.randint(seeds[6], (LEV, NY, NX), 0, 32) < 31).astype(jnp.int32), jax.random.fold_in(seeds[6], 1), 0, 1)
    bottom = place_ends(jax.random.randint(seeds[7], (NY, NX), LEV // 4, LEV + 1), jax.random.fold_in(seeds[7], 1), LEV // 4, LEV).astype(jnp.int32)
    return {"tracer": tracer, "east_flow": east_flow, "north_flow": north_flow, "vertical_flow": vertical_flow, "mixing_lateral": mixing_lateral, "mixing_vertical": mixing_vertical, "sea_mask": sea_mask, "bottom": bottom}


def horizontal_step(content, east_speed, diffusion, wet_cells, north_speed):
    west_side = content[..., :-1]
    east_side = content[..., 1:]
    open_faces = wet_cells[..., :-1] * wet_cells[..., 1:]
    flow_east = east_speed[..., :-1]
    flux_east = open_faces * (jnp.maximum(flow_east, 0.0) * west_side + jnp.minimum(flow_east, 0.0) * east_side
                              + 0.5 * (diffusion[..., :-1] + diffusion[..., 1:]) * (west_side - east_side))
    net_east = flux_east[..., 1:] - flux_east[..., :-1]
    interior = content[..., 1:-1]
    wet_inner = wet_cells[..., 1:-1]
    diff_inner = diffusion[..., 1:-1]
    south_side = interior[..., :-1, :]
    north_side = interior[..., 1:, :]
    open_rows = wet_inner[..., :-1, :] * wet_inner[..., 1:, :]
    north_face = north_speed[..., :-1, :]
    flux_north = open_rows * (jnp.maximum(north_face, 0.0) * south_side + jnp.minimum(north_face, 0.0) * north_side
                              + 0.5 * (diff_inner[..., :-1, :] + diff_inner[..., 1:, :]) * (south_side - north_side))
    wall_rows = jnp.zeros_like(flux_north[..., :1, :])
    padded = jnp.concatenate([wall_rows, flux_north, wall_rows], axis=-2)
    net_north = padded[..., 1:, :] - padded[..., :-1, :]
    return interior - wet_inner * (net_east + net_north)


def vertical_step(content, upward, wet_cells):
    upper_cells = content[..., :-1, :, :]
    lower_cells = content[..., 1:, :, :]
    open_faces = wet_cells[:-1] * wet_cells[1:]
    face_speed = upward[:-1]
    flux_up = open_faces * (jnp.maximum(face_speed, 0.0) * lower_cells + jnp.minimum(face_speed, 0.0) * upper_cells)
    return content[..., 1:-1, :, :] + wet_cells[1:-1] * (flux_up[..., 1:, :, :] - flux_up[..., :-1, :, :])


def implicit_mix(content, mixing, wet_cells):
    coupling = mixing[:-1] * wet_cells[:-1] * wet_cells[1:]
    zeroes = jnp.zeros_like(coupling[:1])
    upper_link = jnp.concatenate([zeroes, coupling], axis=0)
    lower_link = jnp.concatenate([coupling, zeroes], axis=0)
    diagonal = 1.0 + upper_link + lower_link
    levels = content.shape[1]
    ratios = []
    values = []
    for level_id in range(levels):
        if level_id == 0:
            divisor = diagonal[0]
            forcing = content[:, 0]
        else:
            divisor = diagonal[level_id] - upper_link[level_id] * ratios[-1]
            forcing = content[:, level_id] + upper_link[level_id] * values[-1]
        ratios.append(lower_link[level_id] / divisor)
        values.append(forcing / divisor)
    solved = [values[-1]]
    for level_id in range(levels - 2, -1, -1):
        solved.append(values[level_id] + ratios[level_id] * solved[-1])
    return jnp.stack(solved[::-1], axis=1)


def pad_levels(array):
    widths = [(0, 0)] * (array.ndim - 3) + [(1, 1), (0, 0), (0, 0)]
    return jnp.pad(array, widths)


def wrapped(array):
    return jnp.concatenate([array[..., -1:], array, array[..., :1]], axis=-1)


def reference(tracer, east_flow, north_flow, vertical_flow, mixing_lateral, mixing_vertical, sea_mask, bottom):
    level_index = lax.broadcasted_iota(jnp.int32, sea_mask.shape, 0)
    wet_cells = sea_mask.astype(jnp.float32) * (level_index < bottom[None]).astype(jnp.float32)
    tracers_now = tracer
    for substep in range(SUB):
        tracers_now = horizontal_step(wrapped(tracers_now), wrapped(east_flow), wrapped(mixing_lateral),
                                      wrapped(wet_cells), north_flow)
    tracers_now = vertical_step(pad_levels(tracers_now), pad_levels(vertical_flow), pad_levels(wet_cells))
    return implicit_mix(tracers_now, mixing_vertical, wet_cells)
```

```python
import jax
import jax.numpy as jnp
from jax import lax
from jax.experimental import pallas as pl
from jax.experimental.pallas import tpu as pltpu

SUB = 3
EDGE = 2 * SUB
SLOT = 6 * SUB
MESH = pl.DeviceIdType.MESH


def shifted(x, amount, axis):
    size = x.shape[axis]
    amount = amount % size
    return x if amount == 0 else pltpu.roll(x, amount, axis)


def stencil(east, north, diff, wet, not_last_row):
    open_e = wet * shifted(wet, -1, 1)
    mid_e = 0.5 * (diff + shifted(diff, -1, 1))
    alpha = open_e * (jnp.maximum(east, 0.0) + mid_e)
    beta = open_e * (mid_e - jnp.minimum(east, 0.0))
    open_n = wet * shifted(wet, -1, 0) * not_last_row
    mid_n = 0.5 * (diff + shifted(diff, -1, 0))
    gamma = open_n * (jnp.maximum(north, 0.0) + mid_n)
    delta = open_n * (mid_n - jnp.minimum(north, 0.0))
    from_west = shifted(alpha, 1, 1)
    from_south = shifted(gamma, 1, 0)
    centre = 1.0 - (alpha + shifted(beta, 1, 1) + gamma + shifted(delta, 1, 0))
    return centre, beta, from_west, delta, from_south


def substep(c, coefs):
    centre, from_east, from_west, from_north, from_south = coefs
    return (
        centre * c
        + from_east * shifted(c, -1, 1)
        + from_west * shifted(c, 1, 1)
        + from_north * shifted(c, -1, 0)
        + from_south * shifted(c, 1, 0)
    )


def kernel(
    tracer, east, north, upward, lateral, vertical, mask, bottom,
    out,
    fields, up, mix, sea, floor, own, send_e, send_w, recv_w, recv_e,
    ghost, link, flow, lat, inv, quot, drag, forced, part,
    coef_out, coef_in, coef_x, part_out, part_in, part_x, back_out, back_in,
    load_sem, send_sem, recv_sem,
):
    levels, rows, lanes = east.shape
    tracers = tracer.shape[0]
    count = tracers + 4
    ie, iw, idf, iwet = tracers, tracers + 1, tracers + 2, tracers + 3
    slots = lanes // SLOT
    planes = -(-levels // slots)
    padded = planes * slots
    last = levels - 1

    gx, gz = lax.axis_index("gx"), lax.axis_index("gz")
    nx, nz = lax.axis_size("gx"), lax.axis_size("gz")
    go_east, go_west = lax.rem(gx + 1, nx), lax.rem(gx + nx - 1, nx)
    lower = gz // (nz // 2)
    sign = 1 - 2 * lower
    inner = ((gz == 1) | (gz == 2)).astype(jnp.int32)
    is_inner, is_outer = inner == 1, inner == 0
    partner = gz + 1 - 2 * lax.rem(gz, 2)
    across = nz - 1 - gz
    ahead = jnp.where(is_inner, across, partner)

    barrier = pltpu.get_barrier_semaphore()
    for dev in ((go_east, gz), (go_west, gz), (gx, partner)):
        pl.semaphore_signal(barrier, inc=1, device_id=dev, device_id_type=MESH)

    @pl.when(is_inner)
    def _():
        pl.semaphore_signal(barrier, inc=1, device_id=(gx, across), device_id_type=MESH)

    def load(n, src, dst):
        return pltpu.make_async_copy(src, dst, load_sem.at[n])

    loads = [
        load(0, mask, sea),
        load(1, bottom, floor),
        load(2, tracer, fields.at[pl.ds(0, tracers), pl.ds(0, levels)]),
        load(3, east, fields.at[ie, pl.ds(0, levels)]),
        load(4, north, fields.at[iw, pl.ds(0, levels)]),
        load(5, lateral, fields.at[idf, pl.ds(0, levels)]),
        load(6, upward, up),
        load(7, vertical, mix),
    ]
    for copy in loads:
        copy.start()

    plane = (rows, lanes)
    zero = jnp.zeros(plane, jnp.float32)
    lane = lax.broadcasted_iota(jnp.int32, plane, 1)
    row = lax.broadcasted_iota(jnp.int32, plane, 0)
    not_last_row = (row < rows - 1).astype(jnp.float32)
    at = lax.rem(lane, SLOT)

    for f in range(count):
        for k in range(levels, padded):
            fields[f, k] = zero

    @pl.when(is_outer)
    def _():
        for n in range(2):
            coef_in[n] = zero
        for n in range(tracers):
            part_in[n] = zero

    @pl.when(gz == 0)
    def _():
        for n in range(3):
            ghost[n] = zero

    @pl.when(gz == nz - 1)
    def _():
        ghost[3] = zero

    loads[0].wait()
    loads[1].wait()
    depth = floor[...]
    first_level = gz * levels

    def wetness(k, carry):
        fields[iwet, k] = jnp.where(first_level + k < depth, sea[k], 0).astype(jnp.float32)
        return carry

    lax.fori_loop(0, levels, wetness, 0, unroll=5)
    for copy in loads[2:]:
        copy.wait()

    def pack(q, carry):
        to_e, to_w = zero, zero
        for f in range(count):
            acc = zero
            for s in range(slots):
                rolled = shifted(fields[f, q * slots + s], SLOT * s + EDGE, 1)
                acc = jnp.where((lane >= SLOT * s) & (lane < SLOT * s + 2 * EDGE), rolled, acc)
            own[f, q] = jnp.where(at < EDGE, acc, shifted(acc, EDGE, 1))
            here = (at >= SUB * f) & (at < SUB * (f + 1))
            to_e = jnp.where(here, shifted(acc, SUB * f - SUB, 1), to_e)
            to_w = jnp.where(here, shifted(acc, SUB * f - EDGE, 1), to_w)
        send_e[q] = to_e
        send_w[q] = to_w
        return carry

    lax.fori_loop(0, planes, pack, 0)

    pl.semaphore_wait(barrier, 3 + inner)

    def remote(n, src, dst, dev):
        return pltpu.make_async_remote_copy(
            src_ref=src, dst_ref=dst, send_sem=send_sem.at[n], recv_sem=recv_sem.at[n],
            device_id=dev, device_id_type=MESH,
        )

    to_east = remote(0, send_e, recv_w, (go_east, gz))
    to_west = remote(1, send_w, recv_e, (go_west, gz))
    below, above = jnp.minimum(gz + 1, nz - 1), jnp.maximum(gz - 1, 0)
    down = [
        remote(2, fields.at[iwet, last], ghost.at[0], (gx, below)),
        remote(3, mix.at[last], ghost.at[1], (gx, below)),
        remote(4, up.at[last], ghost.at[2], (gx, below)),
    ]
    upwards = remote(5, fields.at[iwet, 0], ghost.at[3], (gx, above))
    coef_ahead = remote(6, coef_out, coef_in, (gx, partner))
    coef_across = remote(7, coef_out, coef_x, (gx, across))
    part_ahead = remote(8, part_out, part_in, (gx, partner))
    part_across = remote(9, part_out, part_x, (gx, across))
    back = remote(10, back_out, back_in, (gx, partner))

    to_east.start()
    to_west.start()

    @pl.when(gz < nz - 1)
    def _():
        for copy in down:
            copy.start()

    @pl.when(gz > 0)
    def _():
        upwards.start()

    def faces(k, carry):
        both = fields[iwet, k - 1] * fields[iwet, k]
        link[k] = mix[k - 1] * both
        flow[k] = up[k - 1] * both
        return carry

    lax.fori_loop(1, levels, faces, 0, unroll=4)

    group = 5

    def advance(g, carry):
        for d in range(group):
            k = g * group + d
            coefs = stencil(fields[ie, k], fields[iw, k], fields[idf, k], fields[iwet, k], not_last_row)
            for n in range(tracers):
                c = fields[n, k]
                for _ in range(SUB):
                    c = substep(c, coefs)
                lat[n, k] = c
        return carry

    lax.fori_loop(0, levels // group, advance, 0)

    @pl.when(gz < nz - 1)
    def _():
        upwards.wait_recv()

    @pl.when(gz > 0)
    def _():
        for copy in down:
            copy.wait_recv()

    both = ghost[0] * fields[iwet, 0]
    link[0] = ghost[1] * both
    flow[0] = ghost[2] * both
    both = fields[iwet, last] * ghost[3]
    link[levels] = mix[last] * both
    flow[levels] = up[last] * both

    start = last * lower

    def spot(m):
        i = start + sign * m
        return i, i + lower, i + 1 - lower

    @pl.when(is_inner)
    def _():
        coef_ahead.wait_recv()

    s = coef_in[0]
    for m in range(levels):
        i, out_face, mid_face = spot(m)
        a, b = link[out_face], link[mid_face]
        top = 1.0 + a * s
        rec = 1.0 / (top + b)
        s = top * rec
        inv[m] = rec
        quot[m] = b * rec
        drag[m] = a * rec
    coef_out[0] = s
    coef_out[1] = inv[last]

    @pl.when(is_outer)
    def _():
        coef_ahead.start()

    @pl.when(is_inner)
    def _():
        coef_across.start()

    to_west.wait_recv()
    to_east.wait_recv()

    def edges(q, carry):
        got_e, got_w = recv_e[q], recv_w[q]
        strip = []
        for f in range(count):
            mine = own[f, q]
            mine = jnp.where((at >= EDGE) & (at < EDGE + SUB), shifted(got_e, EDGE - SUB * f, 1), mine)
            mine = jnp.where((at >= EDGE + SUB) & (at < 2 * EDGE), shifted(got_w, EDGE + SUB - SUB * f, 1), mine)
            strip.append(mine)
        coefs = stencil(strip[ie], strip[iw], strip[idf], strip[iwet], not_last_row)
        for n in range(tracers):
            c = strip[n]
            for _ in range(SUB):
                c = substep(c, coefs)
            own[n, q] = jnp.where(at < EDGE, c, shifted(c, -EDGE, 1))
        return carry

    lax.fori_loop(0, planes, edges, 0)
    rim = (lane < SUB) | (lane >= lanes - SUB)
    for k in range(levels):
        q, slot = divmod(k, slots)
        for n in range(tracers):
            lat[n, k] = jnp.where(rim, shifted(own[n, q], -SLOT * slot - EDGE, 1), lat[n, k])

    speed = sign.astype(jnp.float32)
    for m in range(levels):
        i, out_face, mid_face = spot(m)
        v_out, v_mid = speed * flow[out_face], speed * flow[mid_face]
        rec = inv[m]
        keep = rec * (1.0 + jnp.minimum(v_mid, 0.0) - jnp.maximum(v_out, 0.0))
        if m < last:
            nearer = rec * jnp.maximum(v_mid, 0.0)
        if m > 0:
            farther = rec * -jnp.minimum(v_out, 0.0)
        for n in range(tracers):
            f = keep * lat[n, i]
            if m < last:
                f = f + nearer * lat[n, i + sign]
            if m > 0:
                f = f + farther * lat[n, i - sign]
            forced[n, m] = f

    @pl.when(is_inner)
    def _():
        part_ahead.wait_recv()

    i, out_face, _ = spot(0)
    a_first, v_first = link[out_face], jnp.maximum(speed * flow[out_face], 0.0)
    last_i, _, mid_face = spot(last)
    b_last, v_last = link[mid_face], -jnp.minimum(speed * flow[mid_face], 0.0)
    for n in range(tracers):
        p = forced[n, 0] + inv[0] * (part_in[n] + a_first * coef_in[1] * v_first * lat[n, i])
        part[n, 0] = p
        for m in range(1, levels):
            p = forced[n, m] + drag[m] * p
            part[n, m] = p
        part_out[n] = v_last * lat[n, last_i] + b_last * p

    @pl.when(is_outer)
    def _():
        part_ahead.start()
        back.wait_recv()
        for n in range(tracers):
            u = part[n, last] + inv[last] * back_in[n]
            out[n, last_i] = u

    @pl.when(is_inner)
    def _():
        part_across.start()
        coef_across.wait_recv()
        scale = 1.0 / (coef_out[0] + quot[last] * coef_x[0])
        cross = quot[last] * coef_x[1] * v_last
        base = [part[n, last] + cross * lat[n, last_i] for n in range(tracers)]
        part_across.wait_recv()
        for n in range(tracers):
            u = (base[n] + inv[last] * part_x[n]) * scale
            out[n, last_i] = u

    for n in range(tracers):
        u = out[n, last_i]
        for m in range(last - 1, -1, -1):
            u = part[n, m] + quot[m] * u
            out[n, spot(m)[0]] = u
        back_out[n] = v_first * lat[n, i] + a_first * u

    @pl.when(is_inner)
    def _():
        back.start()
        back.wait_send()
        coef_across.wait_send()
        part_across.wait_send()

    @pl.when(is_outer)
    def _():
        coef_ahead.wait_send()
        part_ahead.wait_send()

    to_east.wait_send()
    to_west.wait_send()

    @pl.when(gz < nz - 1)
    def _():
        for copy in down:
            copy.wait_send()

    @pl.when(gz > 0)
    def _():
        upwards.wait_send()


def local(tracer, east, north, upward, lateral, vertical, mask, bottom):
    tracers, levels, rows, lanes = tracer.shape
    planes = -(-levels // (lanes // SLOT))
    padded = planes * (lanes // SLOT)
    count = tracers + 4
    f32 = jnp.float32

    def vmem(*lead, dtype=f32):
        return pltpu.VMEM(tuple(lead) + (rows, lanes), dtype)

    return pl.pallas_call(
        kernel,
        out_shape=jax.ShapeDtypeStruct(tracer.shape, tracer.dtype),
        in_specs=[pl.BlockSpec(memory_space=pl.ANY)] * 8,
        out_specs=pl.BlockSpec(memory_space=pltpu.VMEM),
        scratch_shapes=[
            vmem(count, padded), vmem(levels), vmem(levels), vmem(levels, dtype=jnp.int32), vmem(dtype=jnp.int32),
            vmem(count, planes), vmem(planes), vmem(planes), vmem(planes), vmem(planes),
            vmem(4), vmem(levels + 1), vmem(levels + 1), vmem(tracers, levels),
            vmem(levels), vmem(levels), vmem(levels), vmem(tracers, levels), vmem(tracers, levels),
            vmem(2), vmem(2), vmem(2), vmem(tracers), vmem(tracers), vmem(tracers), vmem(tracers), vmem(tracers),
            pltpu.SemaphoreType.DMA((8,)), pltpu.SemaphoreType.DMA((11,)), pltpu.SemaphoreType.DMA((11,)),
        ],
        compiler_params=pltpu.CompilerParams(collective_id=0, has_side_effects=True),
        name="ocean_step",
    )(tracer, east, north, upward, lateral, vertical, mask, bottom)


def solution(mesh):
    volume = jax.P("gz", None, "gx")
    return jax.shard_map(
        local,
        mesh=mesh,
        in_specs=(jax.P(None, "gz", None, "gx"),) + (volume,) * 6 + (jax.P(None, "gx"),),
        out_specs=jax.P(None, "gz", None, "gx"),
        check_vma=False,
    )
```

```python
import jax
import jax.numpy as jnp
from jax import lax
from jax.experimental import pallas as pl
from jax.experimental.pallas import tpu as pltpu

SUB = 3
EDGE = 2 * SUB
SLOT = 6 * SUB
MESH = pl.DeviceIdType.MESH


def shifted(x, amount, axis):
    size = x.shape[axis]
    amount = amount % size
    return x if amount == 0 else pltpu.roll(x, amount, axis)


def stencil(east, north, diff, wet, not_last_row):
    open_e = wet * shifted(wet, -1, 1)
    mid_e = 0.5 * (diff + shifted(diff, -1, 1))
    alpha = open_e * (jnp.maximum(east, 0.0) + mid_e)
    beta = open_e * (mid_e - jnp.minimum(east, 0.0))
    open_n = wet * shifted(wet, -1, 0) * not_last_row
    mid_n = 0.5 * (diff + shifted(diff, -1, 0))
    gamma = open_n * (jnp.maximum(north, 0.0) + mid_n)
    delta = open_n * (mid_n - jnp.minimum(north, 0.0))
    from_west = shifted(alpha, 1, 1)
    from_south = shifted(gamma, 1, 0)
    centre = 1.0 - (alpha + shifted(beta, 1, 1) + gamma + shifted(delta, 1, 0))
    return centre, beta, from_west, delta, from_south


def substep(c, coefs):
    centre, from_east, from_west, from_north, from_south = coefs
    return (
        centre * c
        + from_east * shifted(c, -1, 1)
        + from_west * shifted(c, 1, 1)
        + from_north * shifted(c, -1, 0)
        + from_south * shifted(c, 1, 0)
    )


def kernel(
    tracer, east, north, upward, lateral, vertical, mask, bottom,
    out,
    fields, up, mix, sea, floor, own, send_e, send_w, recv_w, recv_e,
    ghost, link, flow, lat, inv, quot, drag, forced, part,
    coef_out, coef_in, coef_x, part_out, part_in, part_x, back_out, back_in,
    load_sem, send_sem, recv_sem, go_sem,
):
    levels, rows, lanes = east.shape
    tracers = tracer.shape[0]
    count = tracers + 4
    ie, iw, idf, iwet = tracers, tracers + 1, tracers + 2, tracers + 3
    slots = lanes // SLOT
    planes = -(-levels // slots)
    padded = planes * slots
    last = levels - 1

    gx, gz = lax.axis_index("gx"), lax.axis_index("gz")
    nx, nz = lax.axis_size("gx"), lax.axis_size("gz")
    go_east, go_west = lax.rem(gx + 1, nx), lax.rem(gx + nx - 1, nx)
    lower = gz // (nz // 2)
    sign = 1 - 2 * lower
    inner = ((gz == 1) | (gz == 2)).astype(jnp.int32)
    is_inner, is_outer = inner == 1, inner == 0
    partner = gz + 1 - 2 * lax.rem(gz, 2)
    across = nz - 1 - gz

    hub = (nz - 1) * lower

    barrier = pltpu.get_barrier_semaphore()

    def greet(sem, dev):
        pl.semaphore_signal(sem, inc=1, device_id=dev, device_id_type=MESH)

    greet(barrier, (go_east, hub))
    greet(barrier, (go_west, hub))

    @pl.when(is_inner)
    def _():
        greet(barrier, (gx, across))
        greet(barrier, (gx, partner))

    def load(n, src, dst):
        return pltpu.make_async_copy(src, dst, load_sem.at[n])

    loads = [
        load(0, mask, sea),
        load(1, bottom, floor),
        load(2, tracer, fields.at[pl.ds(0, tracers), pl.ds(0, levels)]),
        load(3, east, fields.at[ie, pl.ds(0, levels)]),
        load(4, north, fields.at[iw, pl.ds(0, levels)]),
        load(5, lateral, fields.at[idf, pl.ds(0, levels)]),
        load(6, upward, up),
        load(7, vertical, mix),
    ]
    for copy in loads:
        copy.start()

    plane = (rows, lanes)
    zero = jnp.zeros(plane, jnp.float32)
    lane = lax.broadcasted_iota(jnp.int32, plane, 1)
    row = lax.broadcasted_iota(jnp.int32, plane, 0)
    not_last_row = (row < rows - 1).astype(jnp.float32)
    at = lax.rem(lane, SLOT)

    for f in range(count):
        for k in range(levels, padded):
            fields[f, k] = zero

    @pl.when(is_outer)
    def _():
        for n in range(2):
            coef_in[n] = zero
        for n in range(tracers):
            part_in[n] = zero

    @pl.when(gz == 0)
    def _():
        for n in range(3):
            ghost[n] = zero

    @pl.when(gz == nz - 1)
    def _():
        ghost[3] = zero

    loads[0].wait()
    loads[1].wait()
    depth = floor[...]
    first_level = gz * levels

    def wetness(k, carry):
        fields[iwet, k] = jnp.where(first_level + k < depth, sea[k], 0).astype(jnp.float32)
        return carry

    lax.fori_loop(0, levels, wetness, 0, unroll=5)
    for copy in loads[2:]:
        copy.wait()

    turned = [(lane + (lanes - SUB * f)) & (lanes - 1) for f in range(count)]
    owner_e, owner_w = [
        jnp.where(t < slots * SLOT, lax.rem(t // SUB, count), count)
        for t in ((lane + (lanes - SUB)) & (lanes - 1), (lane + (lanes - EDGE)) & (lanes - 1))
    ]
    for q in range(planes):
        to_e, to_w = zero, zero
        for f in range(count):
            acc = shifted(fields[f, q * slots], EDGE + SUB * f, 1)
            for s in range(1, slots):
                rolled = shifted(fields[f, q * slots + s], SLOT * s + EDGE + SUB * f, 1)
                acc = jnp.where(turned[f] >= SLOT * s, rolled, acc)
            own[f, q] = acc
            to_e = jnp.where(owner_e == f, acc, to_e)
            to_w = jnp.where(owner_w == f, acc, to_w)
        send_e[q] = to_e
        send_w[q] = to_w

    @pl.when(is_outer)
    def _():
        pl.semaphore_wait(barrier, 5)
        greet(go_sem, (gx, partner))

    @pl.when(is_inner)
    def _():
        pl.semaphore_wait(go_sem, 1)

    def remote(n, src, dst, dev):
        return pltpu.make_async_remote_copy(
            src_ref=src, dst_ref=dst, send_sem=send_sem.at[n], recv_sem=recv_sem.at[n],
            device_id=dev, device_id_type=MESH,
        )

    to_east = remote(0, send_e, recv_w, (go_east, gz))
    to_west = remote(1, send_w, recv_e, (go_west, gz))
    below, above = jnp.minimum(gz + 1, nz - 1), jnp.maximum(gz - 1, 0)
    down = [
        remote(2, fields.at[iwet, last], ghost.at[0], (gx, below)),
        remote(3, mix.at[last], ghost.at[1], (gx, below)),
        remote(4, up.at[last], ghost.at[2], (gx, below)),
    ]
    upwards = remote(5, fields.at[iwet, 0], ghost.at[3], (gx, above))
    coef_ahead = remote(6, coef_out, coef_in, (gx, partner))
    coef_across = remote(7, coef_out, coef_x, (gx, across))
    part_ahead = remote(8, part_out, part_in, (gx, partner))
    part_across = remote(9, part_out, part_x, (gx, across))
    back = remote(10, back_out, back_in, (gx, partner))

    to_east.start()
    to_west.start()

    for q in range(planes):
        for f in range(count):
            acc = own[f, q]
            own[f, q] = jnp.where(at < EDGE, shifted(acc, -SUB * f, 1), shifted(acc, EDGE - SUB * f, 1))

    @pl.when(is_inner)
    def _():
        pl.semaphore_wait(barrier, 1)

    @pl.when(gz < nz - 1)
    def _():
        for copy in down:
            copy.start()

    @pl.when(gz > 0)
    def _():
        upwards.start()

    def faces(k, carry):
        both = fields[iwet, k - 1] * fields[iwet, k]
        link[k] = mix[k - 1] * both
        flow[k] = up[k - 1] * both
        return carry

    lax.fori_loop(1, levels, faces, 0, unroll=4)

    group = 5

    def advance(g, carry):
        for d in range(group):
            k = g * group + d
            coefs = stencil(fields[ie, k], fields[iw, k], fields[idf, k], fields[iwet, k], not_last_row)
            for n in range(tracers):
                c = fields[n, k]
                for _ in range(SUB):
                    c = substep(c, coefs)
                lat[n, k] = c
        return carry

    lax.fori_loop(0, levels // group, advance, 0)

    @pl.when(gz < nz - 1)
    def _():
        upwards.wait_recv()

    @pl.when(gz > 0)
    def _():
        for copy in down:
            copy.wait_recv()

    both = ghost[0] * fields[iwet, 0]
    link[0] = ghost[1] * both
    flow[0] = ghost[2] * both
    both = fields[iwet, last] * ghost[3]
    link[levels] = mix[last] * both
    flow[levels] = up[last] * both

    start = last * lower

    def spot(m):
        i = start + sign * m
        return i, i + lower, i + 1 - lower

    @pl.when(is_inner)
    def _():
        coef_ahead.wait_recv()

    s = coef_in[0]
    for m in range(levels):
        i, out_face, mid_face = spot(m)
        a, b = link[out_face], link[mid_face]
        top = 1.0 + a * s
        rec = 1.0 / (top + b)
        s = top * rec
        inv[m] = rec
        quot[m] = b * rec
        drag[m] = a * rec
    coef_out[0] = s
    coef_out[1] = inv[last]

    @pl.when(is_outer)
    def _():
        coef_ahead.start()

    @pl.when(is_inner)
    def _():
        coef_across.start()

    to_west.wait_recv()
    to_east.wait_recv()

    def edges(q, carry):
        got_e, got_w = recv_e[q], recv_w[q]
        strip = []
        for f in range(count):
            mine = own[f, q]
            mine = jnp.where((at >= EDGE) & (at < EDGE + SUB), shifted(got_e, -SUB * f, 1), mine)
            mine = jnp.where((at >= EDGE + SUB) & (at < 2 * EDGE), shifted(got_w, EDGE - SUB * f, 1), mine)
            strip.append(mine)
        coefs = stencil(strip[ie], strip[iw], strip[idf], strip[iwet], not_last_row)
        for n in range(tracers):
            c = strip[n]
            for _ in range(SUB):
                c = substep(c, coefs)
            own[n, q] = jnp.where(at < EDGE, c, shifted(c, -EDGE, 1))
        return carry

    lax.fori_loop(0, planes, edges, 0, unroll=True)
    rim = (lane < SUB) | (lane >= lanes - SUB)
    for k in range(levels):
        q, slot = divmod(k, slots)
        for n in range(tracers):
            lat[n, k] = jnp.where(rim, shifted(own[n, q], -SLOT * slot - EDGE, 1), lat[n, k])

    speed = sign.astype(jnp.float32)
    for m in range(levels):
        i, out_face, mid_face = spot(m)
        v_out, v_mid = speed * flow[out_face], speed * flow[mid_face]
        rec = inv[m]
        keep = rec * (1.0 + jnp.minimum(v_mid, 0.0) - jnp.maximum(v_out, 0.0))
        if m < last:
            nearer = rec * jnp.maximum(v_mid, 0.0)
        if m > 0:
            farther = rec * -jnp.minimum(v_out, 0.0)
        for n in range(tracers):
            f = keep * lat[n, i]
            if m < last:
                f = f + nearer * lat[n, i + sign]
            if m > 0:
                f = f + farther * lat[n, i - sign]
            forced[n, m] = f

    @pl.when(is_inner)
    def _():
        part_ahead.wait_recv()

    i, out_face, _ = spot(0)
    a_first, v_first = link[out_face], jnp.maximum(speed * flow[out_face], 0.0)
    last_i, _, mid_face = spot(last)
    b_last, v_last = link[mid_face], -jnp.minimum(speed * flow[mid_face], 0.0)
    for n in range(tracers):
        p = forced[n, 0] + inv[0] * (part_in[n] + a_first * coef_in[1] * v_first * lat[n, i])
        part[n, 0] = p
        for m in range(1, levels):
            p = forced[n, m] + drag[m] * p
            part[n, m] = p
        part_out[n] = v_last * lat[n, last_i] + b_last * p

    @pl.when(is_outer)
    def _():
        part_ahead.start()
        back.wait_recv()
        for n in range(tracers):
            u = part[n, last] + inv[last] * back_in[n]
            out[n, last_i] = u

    @pl.when(is_inner)
    def _():
        part_across.start()
        coef_across.wait_recv()
        scale = 1.0 / (coef_out[0] + quot[last] * coef_x[0])
        cross = quot[last] * coef_x[1] * v_last
        base = [part[n, last] + cross * lat[n, last_i] for n in range(tracers)]
        part_across.wait_recv()
        for n in range(tracers):
            u = (base[n] + inv[last] * part_x[n]) * scale
            out[n, last_i] = u

    for n in range(tracers):
        u = out[n, last_i]
        for m in range(last - 1, -1, -1):
            u = part[n, m] + quot[m] * u
            out[n, spot(m)[0]] = u
        back_out[n] = v_first * lat[n, i] + a_first * u

    @pl.when(is_inner)
    def _():
        back.start()
        back.wait_send()
        coef_across.wait_send()
        part_across.wait_send()

    @pl.when(is_outer)
    def _():
        coef_ahead.wait_send()
        part_ahead.wait_send()

    to_east.wait_send()
    to_west.wait_send()

    @pl.when(gz < nz - 1)
    def _():
        for copy in down:
            copy.wait_send()

    @pl.when(gz > 0)
    def _():
        upwards.wait_send()


def local(tracer, east, north, upward, lateral, vertical, mask, bottom):
    tracers, levels, rows, lanes = tracer.shape
    planes = -(-levels // (lanes // SLOT))
    padded = planes * (lanes // SLOT)
    count = tracers + 4
    f32 = jnp.float32

    def vmem(*lead, dtype=f32):
        return pltpu.VMEM(tuple(lead) + (rows, lanes), dtype)

    return pl.pallas_call(
        kernel,
        out_shape=pltpu.VMEM(tracer.shape, tracer.dtype),
        in_specs=[pl.BlockSpec(memory_space=pl.ANY)] * 8,
        out_specs=pl.BlockSpec(memory_space=pltpu.VMEM),
        scratch_shapes=[
            vmem(count, padded), vmem(levels), vmem(levels), vmem(levels, dtype=jnp.int32), vmem(dtype=jnp.int32),
            vmem(count, planes), vmem(planes), vmem(planes), vmem(planes), vmem(planes),
            vmem(4), vmem(levels + 1), vmem(levels + 1), vmem(tracers, levels),
            vmem(levels), vmem(levels), vmem(levels), vmem(tracers, levels), vmem(tracers, levels),
            vmem(2), vmem(2), vmem(2), vmem(tracers), vmem(tracers), vmem(tracers), vmem(tracers), vmem(tracers),
            pltpu.SemaphoreType.DMA((8,)), pltpu.SemaphoreType.DMA((11,)), pltpu.SemaphoreType.DMA((11,)),
            pltpu.SemaphoreType.REGULAR,
        ],
        compiler_params=pltpu.CompilerParams(collective_id=0, has_side_effects=True),
        name="ocean_step",
    )(tracer, east, north, upward, lateral, vertical, mask, bottom)


def solution(mesh):
    volume = jax.P("gz", None, "gx")
    return jax.shard_map(
        local,
        mesh=mesh,
        in_specs=(jax.P(None, "gz", None, "gx"),) + (volume,) * 6 + (jax.P(None, "gx"),),
        out_specs=jax.P(None, "gz", None, "gx"),
        check_vma=False,
    )
```
